32 devices in a mesh: row: 8 (over y, x, core), col: 4 (over z).
Axes of the slice: x: 2, y: 2, z: 4, core: 2. Of those that a mesh axis runs over, the one named last changes fastest.
Arguments:
- hessenberg: float32 [16384, 16384], P('row', 'col'), may hold values from -6 to 6, as said below
- factors: float32 [3, 32, 512, 512], P(None, 'row', 'col'), may hold values from -1 to 1, as said below
- active: int32 [3, 32], replicated, may hold values 0 or 1
Outputs:
- updated_slab: float32 [16384, 16384], P('row', 'col')
The draws below stay inside these ranges and needn't reach their ends.
Inputs may be any that keep to these rules, and one draw needn't show every extreme that they name: `hessenberg`: in global order, zero below the first subdiagonal. Each factors[f, s] is orthogonal up to float32 rounding.
All inputs are finite; a program needn't handle non-finite values.
Results may differ from the reference program's by a relative error of at most 0.0001.
Values sent between devices are 32-bit elements; how exact they have to be, the bound alone decides.
No kernel may reach another device: no remote copies, remote signals or barrier semaphores. Data moves between devices by JAX's collectives and lax.ppermute only.
A program may use at most 256 MiB of HBM per device.

```python
import math
import jax
import jax.numpy as jnp
from jax import lax

ORDER = 16384
WIN = 512
PHASES = 3
NBLK = 32
N_ROW = 8
N_COL = 4


def draw_hessenberg(key, part):
    row_blocks = ORDER // WIN // N_ROW
    col_blocks = ORDER // WIN // N_COL
    values = jnp.clip(jax.random.normal(key, (ORDER, ORDER), jnp.float32), -6.0, 6.0)
    stored = jnp.arange(ORDER, dtype=jnp.int32)
    glob_row = (stored % (row_blocks * WIN) // WIN * N_ROW + stored // (row_blocks * WIN)) * WIN + stored % WIN
    glob_col = (stored % (col_blocks * WIN) // WIN * N_COL + stored // (col_blocks * WIN)) * WIN + stored % WIN
    return jnp.where(glob_row[:, None] <= glob_col[None, :] + 1, values, 0.0).astype(jnp.float32)


def draw_factors(key, part):
    spread = 0.3
    gaussian = jax.random.normal(key, (PHASES, ORDER // WIN, WIN, WIN), jnp.float32)
    unit_mat = jnp.eye(WIN, dtype=jnp.float32)
    iterate = (unit_mat + spread * gaussian / math.sqrt(WIN)) / 1.8
    for repeat in range(14):
        gram_mat = jnp.einsum('pkab,pkcb->pkac', iterate, iterate, precision=lax.Precision.HIGHEST)
        iterate = 1.5 * iterate - 0.5 * jnp.einsum('pkac,pkcb->pkab', gram_mat, iterate, precision=lax.Precision.HIGHEST)
    mirror = jax.random.normal(jax.random.fold_in(key, 7), (PHASES, ORDER // WIN, WIN), jnp.float32)
    mirror = mirror / jnp.sqrt(jnp.sum(mirror * mirror, axis=-1, keepdims=True))
    image = jnp.einsum('pkab,pkb->pka', iterate, mirror, precision=lax.Precision.HIGHEST)
    iterate = iterate - 2.0 * image[..., :, None] * mirror[..., None, :]
    return iterate.astype(jnp.float32)


def set_ends(array, rng, least, high):
    longest = array.shape.index(max(array.shape))
    spots = []
    for shift in (0, 1):
        where = [jax.random.randint(jax.random.fold_in(rng, axis), (), 0, length) for axis, length in enumerate(array.shape)]
        where[longest] = (where[longest] + shift) % array.shape[longest]
        spots.append(tuple(where))
    return array.at[spots[0]].set(least).at[spots[1]].set(high)


def setup_inputs(seed: int = 0) -> dict:
    arg_keys = jax.random.split(jax.random.key(seed), 4)
    return {
        "hessenberg": draw_hessenberg(jax.random.fold_in(arg_keys[3], 71), 0),
        "factors": draw_factors(jax.random.fold_in(arg_keys[3], 71), 0),
        "active": set_ends((jax.random.randint(arg_keys[2], (PHASES, NBLK), 0, 4) < 3).astype(jnp.int32), jax.random.fold_in(arg_keys[2], 1), 0, 1),
    }


PRECISE = lax.Precision.HIGHEST


def to_global(stored):
    row_blocks = NBLK // N_ROW
    col_blocks = NBLK // N_COL
    matrix = stored.reshape(N_ROW, row_blocks, WIN, ORDER).transpose(1, 0, 2, 3).reshape(ORDER, ORDER)
    return matrix.reshape(ORDER, N_COL, col_blocks, WIN).transpose(0, 2, 1, 3).reshape(ORDER, ORDER)


def to_stored(matrix):
    row_blocks = NBLK // N_ROW
    col_blocks = NBLK // N_COL
    stored = matrix.reshape(row_blocks, N_ROW, WIN, ORDER).transpose(1, 0, 2, 3).reshape(ORDER, ORDER)
    return stored.reshape(ORDER, col_blocks, N_COL, WIN).transpose(0, 2, 1, 3).reshape(ORDER, ORDER)


def reference(hessenberg, factors, active):
    row_blocks = NBLK // N_ROW
    matrix = to_global(hessenberg)
    natural = factors.reshape(PHASES, N_ROW, row_blocks, WIN, WIN).transpose(0, 2, 1, 3, 4).reshape(PHASES, NBLK, WIN, WIN)
    identity = jnp.eye(WIN, dtype=jnp.float32)
    indices = jnp.arange(ORDER, dtype=jnp.int32)
    for phase_idx in range(PHASES):
        offset = (phase_idx % 2) * (WIN // 2)
        win_count = NBLK - (phase_idx % 2)
        win_flags = active[phase_idx, :win_count]
        windows = jnp.where(win_flags[:, None, None] > 0, natural[phase_idx, :win_count], identity)
        slots = jnp.arange(win_count, dtype=jnp.int32)
        win_ends = offset + (slots + 1) * WIN
        window_rows = matrix[offset:offset + win_count * WIN].reshape(win_count, WIN, ORDER)
        updated = jnp.einsum("kab,kan->kbn", windows, window_rows, precision=PRECISE)
        keep_mask = indices[None, :] >= win_ends[:, None]
        window_rows = jnp.where(keep_mask[:, None, :], updated, window_rows)
        matrix = jnp.concatenate([matrix[:offset], window_rows.reshape(win_count * WIN, ORDER), matrix[offset + win_count * WIN:]], axis=0)
        win_starts = offset + slots * WIN
        window_cols = matrix[:, offset:offset + win_count * WIN].reshape(ORDER, win_count, WIN)
        updated = jnp.einsum("nka,kab->nkb", window_cols, windows, precision=PRECISE)
        keep_mask = indices[:, None] < win_starts[None, :]
        window_cols = jnp.where(keep_mask[:, :, None], updated, window_cols)
        matrix = jnp.concatenate([matrix[:, :offset], window_cols.reshape(ORDER, win_count * WIN), matrix[:, offset + win_count * WIN:]], axis=1)
    return to_stored(matrix)
```

```python
import jax
import jax.numpy as jnp
from jax import lax
from jax.experimental import pallas as pl
from jax.experimental.pallas import tpu as pltpu
from jax.sharding import PartitionSpec as P


F32 = jnp.float32
BF16 = jnp.bfloat16


def split(x):
    hi = x.astype(BF16)
    return hi, (x - hi.astype(F32)).astype(BF16)


def mul(left, right):
    (lh, ll), (rh, rl) = left, right
    return lax.dot_general(
        jnp.concatenate([lh, lh, ll], axis=1),
        jnp.concatenate([rh, rl, rh], axis=0),
        (((1,), (0,)), ((), ())),
        preferred_element_type=F32,
    )


def call(kernel, grid, in_specs, out_specs, out_shape, scratch, flops, moved, aliases=None):
    return pl.pallas_call(
        kernel,
        grid_spec=pltpu.PrefetchScalarGridSpec(
            num_scalar_prefetch=1,
            grid=(grid,),
            in_specs=in_specs,
            out_specs=out_specs,
            scratch_shapes=scratch,
        ),
        out_shape=out_shape,
        input_output_aliases=aliases or {},
        cost_estimate=pl.CostEstimate(
            flops=int(flops), bytes_accessed=int(moved), transcendentals=0
        ),
    )


def shape(dims, dtype=F32):
    return jax.ShapeDtypeStruct(dims, dtype)


class Plan:
    def __init__(self, rows, cols, win, grid_rows, grid_cols):
        self.win, self.half = win, win // 2
        self.R, self.C = grid_rows, grid_cols
        self.kb, self.mb = rows // win, cols // win
        self.N = self.kb * grid_rows
        self.t = grid_rows // grid_cols
        assert grid_rows % grid_cols == 0 and grid_rows & (grid_rows - 1) == 0

    def first(self, k):
        return k * self.t

    def count(self, k):
        return self.mb - k * self.t


def ring(value, axis, steps):
    size = lax.axis_size(axis)
    return lax.ppermute(value, axis, [(s, (s + steps) % size) for s in range(size)])


def along(value, axis, steps):
    size = lax.axis_size(axis)
    pairs = [(s, s + steps) for s in range(size) if 0 <= s + steps < size]
    return lax.ppermute(value, axis, pairs)


def around(value, axis, steps):
    last = lax.axis_size(axis) - 1
    return lax.ppermute(value, axis, [(last, 0) if steps > 0 else (0, last)])


def swap(value, axis, bit):
    size = lax.axis_size(axis)
    return lax.ppermute(value, axis, [(s, s ^ bit) for s in range(size)])


def flag(s, g, phase, slot):
    return s[2 + phase * g.N + jnp.clip(slot, 0, g.N - 1)] > 0


def column_factors(g, scalars, same, other):
    part = g.win // g.C

    def kernel(s, same_ref, other_ref, hi, lo):
        for at in range(g.R):
            h, z = at // g.C, at % g.C
            spot = s[0] ^ at
            hi_part, lo_part = split(
                jnp.where(spot % 2 == 0, same_ref[spot // 2, 0], other_ref[spot // 2, 0])
            )
            hi[h, z * part : (z + 1) * part, :] = hi_part
            lo[h, z * part : (z + 1) * part, :] = lo_part

    size = g.mb * g.win * g.win * 4
    return call(
        kernel,
        g.kb,
        [pl.BlockSpec((g.R // 2, 1, part, g.win), lambda i, s: (0, i, 0, 0))] * 2,
        [pl.BlockSpec((g.t, g.win, g.win), lambda i, s: (i, 0, 0))] * 2,
        [shape((g.mb, g.win, g.win), BF16)] * 2,
        [],
        size,
        2 * size,
    )(scalars, same, other)


def keep_lower(g, matrix):
    W = g.win
    spots = [(k, m) for k in range(g.kb) for m in range(g.first(k))]
    if not spots:
        return matrix + 0.0

    def kernel(s, h_ref, o_ref):
        o_ref[...] = h_ref[...]

    block = pl.BlockSpec((W, W), lambda i, s: (s[2 * i], s[2 * i + 1]))
    size = len(spots) * W * W
    return call(
        kernel, len(spots), [block], block, shape(matrix.shape), [], size, 8 * size
    )(jnp.asarray(spots, jnp.int32).reshape(-1), matrix)


def even_first(g, k, scalars, matrix, row_factor, col_hi, col_lo):
    W, half, lo_m, n = g.win, g.half, g.first(k), g.count(k)

    def kernel(s, h_ref, q_ref, ch, cl, left, later, right, qh, ql, x):
        i = pl.program_id(0)
        r, c = k * g.R + s[0], (lo_m + i) * g.C + s[1]
        upper = c > r

        @pl.when(i == 0)
        def _():
            qh[...], ql[...] = split(q_ref[0].T)

        do_left = upper & flag(s, g, 0, r)
        do_right = upper & flag(s, g, 0, c)

        @pl.when(do_left)
        def _():
            x[...] = mul((qh[...], ql[...]), split(h_ref[...]))

        @pl.when(jnp.logical_not(do_left))
        def _():
            x[...] = h_ref[...]

        @pl.when(do_right)
        def _():
            y = mul(split(x[...]), (ch[0], cl[0]))
            left[0] = y[:, :half]
            right[0] = y[:, half:]

            @pl.when(i > 0)
            def _():
                later[0] = y[:, :half]

        @pl.when(jnp.logical_not(do_right))
        def _():
            left[0] = x[:, :half]
            right[0] = x[:, half:]

            @pl.when(i > 0)
            def _():
                later[0] = x[:, :half]

    return call(
        kernel,
        n,
        [
            pl.BlockSpec((W, W), lambda i, s: (k, lo_m + i)),
            pl.BlockSpec((1, W, W), lambda i, s: (k, 0, 0)),
            pl.BlockSpec((1, W, W), lambda i, s: (lo_m + i, 0, 0)),
            pl.BlockSpec((1, W, W), lambda i, s: (lo_m + i, 0, 0)),
        ],
        [
            pl.BlockSpec((1, W, half), lambda i, s: (i, 0, 0)),
            pl.BlockSpec((1, W, half), lambda i, s: (jnp.maximum(i - 1, 0), 0, 0)),
            pl.BlockSpec((1, W, half), lambda i, s: (i, 0, 0)),
        ],
        [shape((n, W, half)), shape((max(n - 1, 1), W, half)), shape((n, W, half))],
        [pltpu.VMEM((W, W), BF16), pltpu.VMEM((W, W), BF16), pltpu.VMEM((W, W), F32)],
        12 * n * W**3,
        12 * n * W * W,
    )(scalars, matrix, row_factor, col_hi, col_lo)


def odd_right(g, k, scalars, right, beyond, round_end, col_hi, col_lo):
    W, half, lo_m, n = g.win, g.half, g.first(k), g.count(k)
    few = max(n - 1, 1)

    def kernel(s, r_ref, b_ref, e_ref, ch, cl, lt, lb, lt_end, lb_end, rt, rb):
        i = pl.program_id(0)
        r, c = k * g.R + s[0], (lo_m + i) * g.C + s[1]
        at_end = s[1] == g.C - 1
        do = (c < g.N - 1) & (r <= c) & flag(s, g, 1, c)

        def theirs(rows):
            return jnp.where(at_end, e_ref[0, rows], b_ref[0, rows])

        @pl.when(do)
        def _():
            x = jnp.concatenate([r_ref[0], theirs(slice(0, W))], axis=1)
            y = mul(split(x), (ch[0], cl[0]))
            rt[0] = y[:half, :half]
            lt[0] = y[:half, half:]
            rb[0] = y[half:, :half]
            lb[0] = y[half:, half:]

        @pl.when(jnp.logical_not(do))
        def _():
            rt[0] = r_ref[0, :half]
            lt[0] = theirs(slice(0, half))

        @pl.when(jnp.logical_not(do) | (r == c))
        def _():
            rb[0] = r_ref[0, half:]
            lb[0] = theirs(slice(half, W))

        @pl.when(i < few)
        def _():
            lt_end[0] = lt[0]
            lb_end[0] = lb[0]

    whole = pl.BlockSpec((1, half, half), lambda i, s: (i, 0, 0))
    part = pl.BlockSpec((1, half, half), lambda i, s: (jnp.minimum(i, few - 1), 0, 0))
    return call(
        kernel,
        n,
        [
            pl.BlockSpec((1, W, half), lambda i, s: (i, 0, 0)),
            pl.BlockSpec((1, W, half), lambda i, s: (jnp.where(s[1] == g.C - 1, 0, i), 0, 0)),
            pl.BlockSpec(
                (1, W, half),
                lambda i, s: (jnp.where(s[1] == g.C - 1, jnp.minimum(i, few - 1), 0), 0, 0),
            ),
            pl.BlockSpec((1, W, W), lambda i, s: (lo_m + i, 0, 0)),
            pl.BlockSpec((1, W, W), lambda i, s: (lo_m + i, 0, 0)),
        ],
        [whole, whole, part, part, whole, whole],
        [shape((m, half, half)) for m in (n, n, few, few, n, n)],
        [],
        6 * n * W**3,
        12 * n * W * W,
    )(scalars, right, beyond, round_end, col_hi, col_lo)


def finish(g, k, scalars, matrix, factors, col_hi, col_lo, own, below, above, out):
    W, half, lo_m, n = g.win, g.half, g.first(k), g.count(k)
    this, prior, last = factors

    def spec(source, wanted=None):
        size, start = g.count(source), g.first(source)

        def index(i, s):
            at = jnp.clip(lo_m + i - start, 0, size - 1)
            if wanted is not None:
                at = jnp.where(wanted(s), at, 0)
            return (at, 0, 0)

        return pl.BlockSpec((1, half, half), index)

    bottom_edge = lambda s: s[0] == g.R - 1
    top_edge = lambda s: s[0] == 0
    has_next, has_prev = below[1] is not None, above[1] is not None

    def kernel(s, h_ref, q1, qp, q2, ch, cl, lt, lb, rt, rb, *rest):
        rest = list(rest)
        take = lambda: (rest.pop(0), rest.pop(0))
        below_here, above_here = take(), take()
        below_next = take() if has_next else below_here
        above_prev = take() if has_prev else above_here
        rest.pop(0)
        o_ref, bh, bl, th, tl, qh, ql, x = rest
        i = pl.program_id(0)
        r, c = k * g.R + s[0], (lo_m + i) * g.C + s[1]

        @pl.when(i == 0)
        def _():
            bh[...], bl[...] = split(q1[0].T[:half])
            th[...], tl[...] = split(qp[0].T)
            qh[...], ql[...] = split(q2[0].T)

        @pl.when(c < r)
        def _():
            o_ref[...] = h_ref[...]

        @pl.when(c >= r)
        def _():
            x[:half, :half] = lt[0]
            x[:half, half:] = rt[0]
            x[half:, :half] = lb[0]
            x[half:, half:] = rb[0]
            do_top = (r > 0) & flag(s, g, 1, r - 1)
            do_bottom = (r < g.N - 1) & (c > r) & flag(s, g, 1, r)

            def top(pair):
                upper = jnp.concatenate([pair[0][0], pair[1][0]], axis=1)
                lower = jnp.concatenate([lt[0], rt[0]], axis=1)
                y = mul((th[...], tl[...]), split(jnp.concatenate([upper, lower], axis=0)))
                x[:half, :] = y

            def bottom(pair):
                upper = jnp.concatenate([lb[0], rb[0]], axis=1)
                lower = jnp.concatenate([pair[0][0], pair[1][0]], axis=1)
                y = mul((bh[...], bl[...]), split(jnp.concatenate([upper, lower], axis=0)))
                x[half:, half:] = y[:, half:]

                @pl.when(c > r + 1)
                def _():
                    x[half:, :half] = y[:, :half]

            edge = top_edge(s)
            if has_prev:
                pl.when(do_top & edge)(lambda: top(above_prev))
            pl.when(do_top & jnp.logical_not(edge))(lambda: top(above_here))
            edge = bottom_edge(s)
            if has_next:
                pl.when(do_bottom & edge)(lambda: bottom(below_next))
            pl.when(do_bottom & jnp.logical_not(edge))(lambda: bottom(below_here))

            @pl.when(c == r)
            def _():
                x[:, :half] = h_ref[:, :half]

            @pl.when((c > r) & flag(s, g, 2, r))
            def _():
                x[...] = mul((qh[...], ql[...]), split(x[...]))

            do_right = (c > r) & flag(s, g, 2, c)

            @pl.when(do_right)
            def _():
                o_ref[...] = mul(split(x[...]), (ch[0], cl[0]))

            @pl.when(jnp.logical_not(do_right))
            def _():
                o_ref[...] = x[...]

    const = lambda i, s: (k, 0, 0)
    column = pl.BlockSpec((1, W, W), lambda i, s: (lo_m + i, 0, 0))
    operands = [matrix, this, prior, last, col_hi, col_lo, *own, *below[0], *above[0]]
    in_specs = [
        pl.BlockSpec((W, W), lambda i, s: (k, lo_m + i)),
        pl.BlockSpec((1, W, W), const),
        pl.BlockSpec(
            (1, W, half),
            lambda i, s: (jnp.maximum(k - jnp.where(s[0] == 0, 1, 0), 0), 0, 0),
        ),
        pl.BlockSpec((1, W, W), const),
        column,
        column,
        spec(k),
        spec(k),
        spec(k),
        spec(k),
        spec(k),
        spec(k),
        spec(k),
        spec(k),
    ]
    if has_next:
        operands += below[1]
        in_specs += [spec(k + 1, bottom_edge), spec(k + 1, bottom_edge)]
    if has_prev:
        operands += above[1]
        in_specs += [spec(k - 1, top_edge), spec(k - 1, top_edge)]
    aliases = {1 + len(operands): 0}
    operands.append(out)
    in_specs.append(pl.BlockSpec(memory_space=pl.ANY))
    return call(
        kernel,
        n,
        in_specs,
        pl.BlockSpec((W, W), lambda i, s: (k, lo_m + i)),
        shape(matrix.shape),
        [pltpu.VMEM((half, W), BF16)] * 4
        + [pltpu.VMEM((W, W), BF16)] * 2
        + [pltpu.VMEM((W, W), F32)],
        18 * n * W**3,
        24 * n * W * W,
        aliases,
    )(scalars, *operands)


def local(hessenberg, factors, active):
    rows_here, cols_here = hessenberg.shape
    phases, _, _, win = factors.shape
    R, C = lax.axis_size("row"), lax.axis_size("col")
    g = Plan(rows_here, cols_here, win, R, C)
    assert phases == 3
    p, q = lax.axis_index("row"), lax.axis_index("col")
    scalars = jnp.concatenate(
        [jnp.stack([p, q]).astype(jnp.int32), active.astype(jnp.int32).reshape(-1)]
    )

    spread = [
        [
            ((h * C + a) * C + a, (h * C + (a + d) % C) * C + a)
            for h in range(g.t)
            for a in range(C)
        ]
        for d in range(C)
    ]
    part = g.win // C

    row_factor, col_factor = [], []
    for f in range(phases):
        row_factor.append(lax.all_gather(factors[f], "col", axis=1, tiled=True))
        cut = [
            lax.dynamic_slice_in_dim(row_factor[f], (q + d) % C * part, part, axis=1)
            for d in range(C)
        ]
        piece = jnp.where(p % C == q, cut[0], 0.0)
        for d in range(1, C):
            piece = piece + lax.ppermute(cut[d], ("row", "col"), spread[d])
        same = [piece]
        for j in range(2, R, 2):
            same.append(swap(piece, "row", j))
        same = jnp.stack(same)
        other = swap(same, "row", 1)
        col_factor.append(column_factors(g, scalars, same, other))
    prior = ring(row_factor[1][:, :, g.half :], "row", 1)

    own, tops, bottoms = [], [], []
    for k in range(g.kb):
        left, later, right = even_first(g, k, scalars, hessenberg, row_factor[0], *col_factor[0])
        beyond = along(left, "col", -1)
        round_end = around(later, "col", -1)
        lt, lb, lt_end, lb_end, rt, rb = odd_right(
            g, k, scalars, right, beyond, round_end, *col_factor[1]
        )
        lt = along(lt, "col", 1)
        lb = along(lb, "col", 1)
        lt_end = around(lt_end, "col", 1)
        lb_end = around(lb_end, "col", 1)
        lt, lb = joined(lt, lt_end), joined(lb, lb_end)
        own.append((lt, lb, rt, rb))
        rt = ring(rt, "row", -1)
        rb = ring(rb, "row", 1)
        lt = ring(lt, "row", -1)
        lb = ring(lb, "row", 1)
        tops.append((lt, rt))
        bottoms.append((lb, rb))
    out = keep_lower(g, hessenberg)
    for k in range(g.kb):
        below = (tops[k], tops[k + 1] if k + 1 < g.kb else None)
        above = (bottoms[k], bottoms[k - 1] if k > 0 else None)
        out = finish(
            g,
            k,
            scalars,
            hessenberg,
            (row_factor[1], prior, row_factor[2]),
            *col_factor[2],
            own[k],
            below,
            above,
            out,
        )
    return out


def joined(straight, end):
    extra = straight.shape[0] - 1
    if not extra:
        return straight
    return straight + jnp.pad(end, ((1, 0), (0, 0), (0, 0)))


def solution(mesh):
    return jax.shard_map(
        local,
        mesh=mesh,
        in_specs=(P("row", "col"), P(None, "row", "col", None), P()),
        out_specs=P("row", "col"),
        check_vma=False,
    )
```

```python
import jax
import jax.numpy as jnp
from jax import lax
from jax.experimental import pallas as pl
from jax.experimental.pallas import tpu as pltpu
from jax.sharding import PartitionSpec as P


F32 = jnp.float32
BF16 = jnp.bfloat16


def split(x):
    hi = x.astype(BF16)
    return hi, (x - hi.astype(F32)).astype(BF16)


def mul(left, right):
    (lh, ll), (rh, rl) = left, right
    return lax.dot_general(
        jnp.concatenate([lh, lh, ll], axis=1),
        jnp.concatenate([rh, rl, rh], axis=0),
        (((1,), (0,)), ((), ())),
        preferred_element_type=F32,
    )


def call(kernel, grid, in_specs, out_specs, out_shape, scratch, flops, moved, aliases=None):
    return pl.pallas_call(
        kernel,
        grid_spec=pltpu.PrefetchScalarGridSpec(
            num_scalar_prefetch=1,
            grid=(grid,),
            in_specs=in_specs,
            out_specs=out_specs,
            scratch_shapes=scratch,
        ),
        out_shape=out_shape,
        input_output_aliases=aliases or {},
        cost_estimate=pl.CostEstimate(
            flops=int(flops), bytes_accessed=int(moved), transcendentals=0
        ),
    )


def shape(dims, dtype=F32):
    return jax.ShapeDtypeStruct(dims, dtype)


class Plan:
    def __init__(self, rows, cols, win, grid_rows, grid_cols):
        self.win, self.half = win, win // 2
        self.R, self.C = grid_rows, grid_cols
        self.kb, self.mb = rows // win, cols // win
        self.N = self.kb * grid_rows
        self.t = grid_rows // grid_cols
        assert grid_rows % grid_cols == 0 and grid_rows & (grid_rows - 1) == 0

    def first(self, k):
        return k * self.t

    def count(self, k):
        return self.mb - k * self.t


def ring(value, axis, steps):
    size = lax.axis_size(axis)
    return lax.ppermute(value, axis, [(s, (s + steps) % size) for s in range(size)])


def along(value, axis, steps):
    size = lax.axis_size(axis)
    pairs = [(s, s + steps) for s in range(size) if 0 <= s + steps < size]
    return lax.ppermute(value, axis, pairs)


def around(value, axis, steps):
    last = lax.axis_size(axis) - 1
    return lax.ppermute(value, axis, [(last, 0) if steps > 0 else (0, last)])


def swap(value, axis, bit):
    size = lax.axis_size(axis)
    return lax.ppermute(value, axis, [(s, s ^ bit) for s in range(size)])


def flag(s, g, phase, slot):
    return s[2 + phase * g.N + jnp.clip(slot, 0, g.N - 1)] > 0


def column_factors(g, scalars, same, other):
    part = g.win // g.C

    def kernel(s, same_ref, other_ref, hi, lo):
        for at in range(g.R):
            h, z = at // g.C, at % g.C
            spot = s[0] ^ at
            hi_part, lo_part = split(
                jnp.where(spot % 2 == 0, same_ref[spot // 2, 0], other_ref[spot // 2, 0])
            )
            hi[h, z * part : (z + 1) * part, :] = hi_part
            lo[h, z * part : (z + 1) * part, :] = lo_part

    size = g.mb * g.win * g.win * 4
    return call(
        kernel,
        g.kb,
        [pl.BlockSpec((g.R // 2, 1, part, g.win), lambda i, s: (0, i, 0, 0))] * 2,
        [pl.BlockSpec((g.t, g.win, g.win), lambda i, s: (i, 0, 0))] * 2,
        [shape((g.mb, g.win, g.win), BF16)] * 2,
        [],
        size,
        2 * size,
    )(scalars, same, other)


def keep_lower(g, matrix):
    W = g.win
    spots = [(k, m) for k in range(g.kb) for m in range(g.first(k))]
    if not spots:
        return matrix + 0.0

    def kernel(s, h_ref, o_ref):
        o_ref[...] = h_ref[...]

    block = pl.BlockSpec((W, W), lambda i, s: (s[2 * i], s[2 * i + 1]))
    size = len(spots) * W * W
    return call(
        kernel, len(spots), [block], block, shape(matrix.shape), [], size, 8 * size
    )(jnp.asarray(spots, jnp.int32).reshape(-1), matrix)


def even_first(g, k, scalars, matrix, row_factor, col_hi, col_lo):
    W, half, lo_m, n = g.win, g.half, g.first(k), g.count(k)

    def kernel(s, h_ref, q_ref, ch, cl, left, later, right, qh, ql, x):
        i = pl.program_id(0)
        r, c = k * g.R + s[0], (lo_m + i) * g.C + s[1]
        upper = c > r

        @pl.when(i == 0)
        def _():
            qh[...], ql[...] = split(q_ref[0, 0].T)

        do_left = upper & flag(s, g, 0, r)
        do_right = upper & flag(s, g, 0, c)

        @pl.when(do_left)
        def _():
            x[...] = mul((qh[...], ql[...]), split(h_ref[...]))

        @pl.when(jnp.logical_not(do_left))
        def _():
            x[...] = h_ref[...]

        @pl.when(do_right)
        def _():
            y = mul(split(x[...]), (ch[0], cl[0]))
            left[0] = y[:, :half]
            right[0] = y[:, half:]

            @pl.when(i > 0)
            def _():
                later[0] = y[:, :half]

        @pl.when(jnp.logical_not(do_right))
        def _():
            left[0] = x[:, :half]
            right[0] = x[:, half:]

            @pl.when(i > 0)
            def _():
                later[0] = x[:, :half]

    return call(
        kernel,
        n,
        [
            pl.BlockSpec((W, W), lambda i, s: (k, lo_m + i)),
            pl.BlockSpec((1, 1, W, W), lambda i, s: (0, k, 0, 0)),
            pl.BlockSpec((1, W, W), lambda i, s: (lo_m + i, 0, 0)),
            pl.BlockSpec((1, W, W), lambda i, s: (lo_m + i, 0, 0)),
        ],
        [
            pl.BlockSpec((1, W, half), lambda i, s: (i, 0, 0)),
            pl.BlockSpec((1, W, half), lambda i, s: (jnp.maximum(i - 1, 0), 0, 0)),
            pl.BlockSpec((1, W, half), lambda i, s: (i, 0, 0)),
        ],
        [shape((n, W, half)), shape((max(n - 1, 1), W, half)), shape((n, W, half))],
        [pltpu.VMEM((W, W), BF16), pltpu.VMEM((W, W), BF16), pltpu.VMEM((W, W), F32)],
        12 * n * W**3,
        12 * n * W * W,
    )(scalars, matrix, row_factor, col_hi, col_lo)


def odd_right(g, k, scalars, right, beyond, round_end, col_hi, col_lo):
    W, half, lo_m, n = g.win, g.half, g.first(k), g.count(k)
    few = max(n - 1, 1)

    def kernel(s, r_ref, b_ref, e_ref, ch, cl, lt, lb, lt_end, lb_end, rt, rb):
        i = pl.program_id(0)
        r, c = k * g.R + s[0], (lo_m + i) * g.C + s[1]
        at_end = s[1] == g.C - 1
        do = (c < g.N - 1) & (r <= c) & flag(s, g, 1, c)

        def theirs(rows):
            return jnp.where(at_end, e_ref[0, rows], b_ref[0, rows])

        @pl.when(do)
        def _():
            x = jnp.concatenate([r_ref[0], theirs(slice(0, W))], axis=1)
            y = mul(split(x), (ch[0], cl[0]))
            rt[0] = y[:half, :half]
            lt[0] = y[:half, half:]
            rb[0] = y[half:, :half]
            lb[0] = y[half:, half:]

        @pl.when(jnp.logical_not(do))
        def _():
            rt[0] = r_ref[0, :half]
            lt[0] = theirs(slice(0, half))

        @pl.when(jnp.logical_not(do) | (r == c))
        def _():
            rb[0] = r_ref[0, half:]
            lb[0] = theirs(slice(half, W))

        @pl.when(i < few)
        def _():
            lt_end[0] = lt[0]
            lb_end[0] = lb[0]

    whole = pl.BlockSpec((1, half, half), lambda i, s: (i, 0, 0))
    part = pl.BlockSpec((1, half, half), lambda i, s: (jnp.minimum(i, few - 1), 0, 0))
    return call(
        kernel,
        n,
        [
            pl.BlockSpec((1, W, half), lambda i, s: (i, 0, 0)),
            pl.BlockSpec((1, W, half), lambda i, s: (jnp.where(s[1] == g.C - 1, 0, i), 0, 0)),
            pl.BlockSpec(
                (1, W, half),
                lambda i, s: (jnp.where(s[1] == g.C - 1, jnp.minimum(i, few - 1), 0), 0, 0),
            ),
            pl.BlockSpec((1, W, W), lambda i, s: (lo_m + i, 0, 0)),
            pl.BlockSpec((1, W, W), lambda i, s: (lo_m + i, 0, 0)),
        ],
        [whole, whole, part, part, whole, whole],
        [shape((m, half, half)) for m in (n, n, few, few, n, n)],
        [],
        6 * n * W**3,
        12 * n * W * W,
    )(scalars, right, beyond, round_end, col_hi, col_lo)


def finish(g, k, scalars, matrix, factors, col_hi, col_lo, own, below, above, out):
    W, half, lo_m, n = g.win, g.half, g.first(k), g.count(k)
    later, prior = factors

    def spec(source, wanted=None):
        size, start = g.count(source), g.first(source)

        def index(i, s):
            at = jnp.clip(lo_m + i - start, 0, size - 1)
            if wanted is not None:
                at = jnp.where(wanted(s), at, 0)
            return (at, 0, 0)

        return pl.BlockSpec((1, half, half), index)

    bottom_edge = lambda s: s[0] == g.R - 1
    top_edge = lambda s: s[0] == 0
    has_next, has_prev = below[1] is not None, above[1] is not None

    def kernel(s, h_ref, q1, qp, q2, ch, cl, lt, lb, rt, rb, *rest):
        rest = list(rest)
        take = lambda: (rest.pop(0), rest.pop(0))
        below_here, above_here = take(), take()
        below_next = take() if has_next else below_here
        above_prev = take() if has_prev else above_here
        rest.pop(0)
        o_ref, bh, bl, th, tl, qh, ql, x = rest
        i = pl.program_id(0)
        r, c = k * g.R + s[0], (lo_m + i) * g.C + s[1]

        @pl.when(i == 0)
        def _():
            bh[...], bl[...] = split(q1[0, 0].T[:half])
            th[...], tl[...] = split(qp[0].T)
            qh[...], ql[...] = split(q2[0, 0].T)

        @pl.when(c < r)
        def _():
            o_ref[...] = h_ref[...]

        @pl.when(c >= r)
        def _():
            x[:half, :half] = lt[0]
            x[:half, half:] = rt[0]
            x[half:, :half] = lb[0]
            x[half:, half:] = rb[0]
            do_top = (r > 0) & flag(s, g, 1, r - 1)
            do_bottom = (r < g.N - 1) & (c > r) & flag(s, g, 1, r)

            def chosen(here, there, edge, has):
                pair = [ref[0] for ref in here]
                if has:
                    pair = [jnp.where(edge, far[0], near) for far, near in zip(there, pair)]
                return jnp.concatenate(pair, axis=1)

            @pl.when(do_top)
            def _():
                upper = chosen(above_here, above_prev, top_edge(s), has_prev)
                lower = jnp.concatenate([lt[0], rt[0]], axis=1)
                y = mul((th[...], tl[...]), split(jnp.concatenate([upper, lower], axis=0)))
                x[:half, :] = y

            @pl.when(do_bottom)
            def _():
                upper = jnp.concatenate([lb[0], rb[0]], axis=1)
                lower = chosen(below_here, below_next, bottom_edge(s), has_next)
                y = mul((bh[...], bl[...]), split(jnp.concatenate([upper, lower], axis=0)))
                x[half:, half:] = y[:, half:]

                @pl.when(c > r + 1)
                def _():
                    x[half:, :half] = y[:, :half]

            @pl.when(c == r)
            def _():
                x[:, :half] = h_ref[:, :half]

            @pl.when((c > r) & flag(s, g, 2, r))
            def _():
                x[...] = mul((qh[...], ql[...]), split(x[...]))

            do_right = (c > r) & flag(s, g, 2, c)

            @pl.when(do_right)
            def _():
                o_ref[...] = mul(split(x[...]), (ch[0], cl[0]))

            @pl.when(jnp.logical_not(do_right))
            def _():
                o_ref[...] = x[...]

    column = pl.BlockSpec((1, W, W), lambda i, s: (lo_m + i, 0, 0))
    operands = [matrix, later, prior, later, col_hi, col_lo, *own, *below[0], *above[0]]
    in_specs = [
        pl.BlockSpec((W, W), lambda i, s: (k, lo_m + i)),
        pl.BlockSpec((1, 1, W, W), lambda i, s: (0, k, 0, 0)),
        pl.BlockSpec(
            (1, W, half),
            lambda i, s: (jnp.maximum(k - jnp.where(s[0] == 0, 1, 0), 0), 0, 0),
        ),
        pl.BlockSpec((1, 1, W, W), lambda i, s: (1, k, 0, 0)),
        column,
        column,
        spec(k),
        spec(k),
        spec(k),
        spec(k),
        spec(k),
        spec(k),
        spec(k),
        spec(k),
    ]
    if has_next:
        operands += below[1]
        in_specs += [spec(k + 1, bottom_edge), spec(k + 1, bottom_edge)]
    if has_prev:
        operands += above[1]
        in_specs += [spec(k - 1, top_edge), spec(k - 1, top_edge)]
    aliases = {1 + len(operands): 0}
    operands.append(out)
    in_specs.append(pl.BlockSpec(memory_space=pl.ANY))
    return call(
        kernel,
        n,
        in_specs,
        pl.BlockSpec((W, W), lambda i, s: (k, lo_m + i)),
        shape(matrix.shape),
        [pltpu.VMEM((half, W), BF16)] * 4
        + [pltpu.VMEM((W, W), BF16)] * 2
        + [pltpu.VMEM((W, W), F32)],
        18 * n * W**3,
        24 * n * W * W,
        aliases,
    )(scalars, *operands)


def local(hessenberg, factors, active):
    rows_here, cols_here = hessenberg.shape
    phases, _, _, win = factors.shape
    R, C = lax.axis_size("row"), lax.axis_size("col")
    g = Plan(rows_here, cols_here, win, R, C)
    assert phases == 3
    p, q = lax.axis_index("row"), lax.axis_index("col")
    scalars = jnp.concatenate(
        [jnp.stack([p, q]).astype(jnp.int32), active.astype(jnp.int32).reshape(-1)]
    )

    spread = [
        [
            ((h * C + a) * C + a, (h * C + (a + d) % C) * C + a)
            for h in range(g.t)
            for a in range(C)
        ]
        for d in range(C)
    ]
    part = g.win // C

    first = lax.all_gather(factors[:1], "col", axis=2, tiled=True)
    odd_last = lax.all_gather(factors[1:], "col", axis=2, tiled=True)

    def columns(source, at, since=None):
        cut = [
            lax.dynamic_slice(
                source, (at, 0, (q + d) % C * part, 0), (1, g.kb, part, g.win)
            )[0]
            for d in range(C)
        ]
        if since is not None:
            *cut, _ = lax.optimization_barrier((*cut, since[0, :8, :128]))
        piece = jnp.where(p % C == q, cut[0], 0.0)
        for d in range(1, C):
            piece = piece + lax.ppermute(cut[d], ("row", "col"), spread[d])
        same = [piece]
        for j in range(2, R, 2):
            same.append(swap(piece, "row", j))
        same = jnp.stack(same)
        other = swap(same, "row", 1)
        return column_factors(g, scalars, same, other)

    col_factor = [columns(first, 0), columns(odd_last, 0)]
    prior = ring(odd_last[0, :, :, g.half :], "row", 1)

    own, tops, bottoms = [], [], []
    for k in range(g.kb):
        left, later, right = even_first(
            g, k, scalars, hessenberg, first, *col_factor[0]
        )
        beyond = along(left, "col", -1)
        round_end = around(later, "col", -1)
        lt, lb, lt_end, lb_end, rt, rb = odd_right(
            g, k, scalars, right, beyond, round_end, *col_factor[1]
        )
        if k == 0:
            col_factor.append(columns(odd_last, 1, rb))
        lt = along(lt, "col", 1)
        lb = along(lb, "col", 1)
        lt_end = around(lt_end, "col", 1)
        lb_end = around(lb_end, "col", 1)
        lt, lb = joined(lt, lt_end), joined(lb, lb_end)
        own.append((lt, lb, rt, rb))
        rt = ring(rt, "row", -1)
        rb = ring(rb, "row", 1)
        lt = ring(lt, "row", -1)
        lb = ring(lb, "row", 1)
        tops.append((lt, rt))
        bottoms.append((lb, rb))
    out = keep_lower(g, hessenberg)
    for k in range(g.kb):
        below = (tops[k], tops[k + 1] if k + 1 < g.kb else None)
        above = (bottoms[k], bottoms[k - 1] if k > 0 else None)
        out = finish(
            g,
            k,
            scalars,
            hessenberg,
            (odd_last, prior),
            *col_factor[2],
            own[k],
            below,
            above,
            out,
        )
    return out


def joined(straight, end):
    extra = straight.shape[0] - 1
    if not extra:
        return straight
    return straight + jnp.pad(end, ((1, 0), (0, 0), (0, 0)))


def solution(mesh):
    return jax.shard_map(
        local,
        mesh=mesh,
        in_specs=(P("row", "col"), P(None, "row", "col", None), P()),
        out_specs=P("row", "col"),
        check_vma=False,
    )
```

```python
import jax
import jax.numpy as jnp
from jax import lax
from jax.experimental import pallas as pl
from jax.experimental.pallas import tpu as pltpu
from jax.sharding import PartitionSpec as P


F32 = jnp.float32
BF16 = jnp.bfloat16


def split(x):
    hi = x.astype(BF16)
    return hi, (x - hi.astype(F32)).astype(BF16)


def mul(left, right):
    (lh, ll), (rh, rl) = left, right
    return lax.dot_general(
        jnp.concatenate([lh, lh, ll], axis=1),
        jnp.concatenate([rh, rl, rh], axis=0),
        (((1,), (0,)), ((), ())),
        preferred_element_type=F32,
    )


def call(kernel, grid, in_specs, out_specs, out_shape, scratch, flops, moved, aliases=None):
    return pl.pallas_call(
        kernel,
        grid_spec=pltpu.PrefetchScalarGridSpec(
            num_scalar_prefetch=1,
            grid=(grid,),
            in_specs=in_specs,
            out_specs=out_specs,
            scratch_shapes=scratch,
        ),
        out_shape=out_shape,
        input_output_aliases=aliases or {},
        cost_estimate=pl.CostEstimate(
            flops=int(flops), bytes_accessed=int(moved), transcendentals=0
        ),
    )


def shape(dims, dtype=F32):
    return jax.ShapeDtypeStruct(dims, dtype)


class Plan:
    def __init__(self, rows, cols, win, grid_rows, grid_cols):
        self.win, self.half = win, win // 2
        self.R, self.C = grid_rows, grid_cols
        self.kb, self.mb = rows // win, cols // win
        self.N = self.kb * grid_rows
        self.t = grid_rows // grid_cols
        assert grid_rows % grid_cols == 0 and grid_rows & (grid_rows - 1) == 0

    def first(self, k):
        return k * self.t

    def count(self, k):
        return self.mb - k * self.t


def ring(value, axis, steps):
    size = lax.axis_size(axis)
    return lax.ppermute(value, axis, [(s, (s + steps) % size) for s in range(size)])


def along(value, axis, steps):
    size = lax.axis_size(axis)
    pairs = [(s, s + steps) for s in range(size) if 0 <= s + steps < size]
    return lax.ppermute(value, axis, pairs)


def around(value, axis, steps):
    last = lax.axis_size(axis) - 1
    return lax.ppermute(value, axis, [(last, 0) if steps > 0 else (0, last)])


def swap(value, axis, bit):
    size = lax.axis_size(axis)
    return lax.ppermute(value, axis, [(s, s ^ bit) for s in range(size)])


def flag(s, g, phase, slot):
    return s[2 + phase * g.N + jnp.clip(slot, 0, g.N - 1)] > 0


def column_factors(g, scalars, same, other):
    part = g.win // g.C

    def kernel(s, same_ref, other_ref, hi, lo):
        for at in range(g.R):
            h, z = at // g.C, at % g.C
            spot = s[0] ^ at
            hi_part, lo_part = split(
                jnp.where(spot % 2 == 0, same_ref[spot // 2, 0], other_ref[spot // 2, 0])
            )
            hi[h, z * part : (z + 1) * part, :] = hi_part
            lo[h, z * part : (z + 1) * part, :] = lo_part

    size = g.mb * g.win * g.win * 4
    return call(
        kernel,
        g.kb,
        [pl.BlockSpec((g.R // 2, 1, part, g.win), lambda i, s: (0, i, 0, 0))] * 2,
        [pl.BlockSpec((g.t, g.win, g.win), lambda i, s: (i, 0, 0))] * 2,
        [shape((g.mb, g.win, g.win), BF16)] * 2,
        [],
        size,
        2 * size,
    )(scalars, same, other)


def keep_lower(g, matrix):
    W = g.win
    spots = [(k, m) for k in range(g.kb) for m in range(g.first(k))]
    if not spots:
        return matrix + 0.0

    def kernel(s, h_ref, o_ref):
        o_ref[...] = h_ref[...]

    block = pl.BlockSpec((W, W), lambda i, s: (s[2 * i], s[2 * i + 1]))
    size = len(spots) * W * W
    return call(
        kernel, len(spots), [block], block, shape(matrix.shape), [], size, 8 * size
    )(jnp.asarray(spots, jnp.int32).reshape(-1), matrix)


def row_factors(g, scalars, source, prior):
    W, half = g.win, g.half

    def kernel(s, q1, qp, q2, bh, bl, th, tl, qh, ql):
        bh[0], bl[0] = split(q1[0, 0].T[:half])
        th[0], tl[0] = split(qp[0].T)
        qh[0], ql[0] = split(q2[0, 0].T)

    part = pl.BlockSpec((1, half, W), lambda i, s: (i, 0, 0))
    size = g.kb * W * W
    return call(
        kernel,
        g.kb,
        [
            pl.BlockSpec((1, 1, W, W), lambda i, s: (0, i, 0, 0)),
            pl.BlockSpec((1, W, half), lambda i, s: (i, 0, 0)),
            pl.BlockSpec((1, 1, W, W), lambda i, s: (1, i, 0, 0)),
        ],
        [part] * 4 + [pl.BlockSpec((1, W, W), lambda i, s: (i, 0, 0))] * 2,
        [shape((g.kb, half, W), BF16)] * 4 + [shape((g.kb, W, W), BF16)] * 2,
        [],
        size,
        20 * size,
    )(scalars, source, prior, source)


def even_first(g, k, scalars, matrix, row_factor, col_hi, col_lo):
    W, half, lo_m, n = g.win, g.half, g.first(k), g.count(k)

    def kernel(s, h_ref, q_ref, ch, cl, left, later, right, qh, ql, x):
        i = pl.program_id(0)
        r, c = k * g.R + s[0], (lo_m + i) * g.C + s[1]
        upper = c > r

        @pl.when(i == 0)
        def _():
            qh[...], ql[...] = split(q_ref[0, 0].T)

        do_left = upper & flag(s, g, 0, r)
        do_right = upper & flag(s, g, 0, c)

        @pl.when(do_left)
        def _():
            x[...] = mul((qh[...], ql[...]), split(h_ref[...]))

        @pl.when(jnp.logical_not(do_left))
        def _():
            x[...] = h_ref[...]

        @pl.when(do_right)
        def _():
            y = mul(split(x[...]), (ch[0], cl[0]))
            left[0] = y[:, :half]
            right[0] = y[:, half:]

        @pl.when(jnp.logical_not(do_right))
        def _():
            left[0] = x[:, :half]
            right[0] = x[:, half:]

        @pl.when(i > 0)
        def _():
            later[0] = left[0]

    return call(
        kernel,
        n,
        [
            pl.BlockSpec((W, W), lambda i, s: (k, lo_m + i)),
            pl.BlockSpec((1, 1, W, W), lambda i, s: (0, k, 0, 0)),
            pl.BlockSpec((1, W, W), lambda i, s: (lo_m + i, 0, 0)),
            pl.BlockSpec((1, W, W), lambda i, s: (lo_m + i, 0, 0)),
        ],
        [
            pl.BlockSpec((1, W, half), lambda i, s: (i, 0, 0)),
            pl.BlockSpec((1, W, half), lambda i, s: (jnp.maximum(i - 1, 0), 0, 0)),
            pl.BlockSpec((1, W, half), lambda i, s: (i, 0, 0)),
        ],
        [shape((n, W, half)), shape((max(n - 1, 1), W, half)), shape((n, W, half))],
        [pltpu.VMEM((W, W), BF16), pltpu.VMEM((W, W), BF16), pltpu.VMEM((W, W), F32)],
        12 * n * W**3,
        12 * n * W * W,
    )(scalars, matrix, row_factor, col_hi, col_lo)


def odd_right(g, k, scalars, right, beyond, round_end, col_hi, col_lo):
    W, half, lo_m, n = g.win, g.half, g.first(k), g.count(k)
    few = max(n - 1, 1)

    def kernel(s, r_ref, b_ref, e_ref, ch, cl, lt, lb, lt_end, lb_end, rt, rb):
        i = pl.program_id(0)
        r, c = k * g.R + s[0], (lo_m + i) * g.C + s[1]
        at_end = s[1] == g.C - 1
        do = (c < g.N - 1) & (r <= c) & flag(s, g, 1, c)

        def theirs(rows):
            return jnp.where(at_end, e_ref[0, rows], b_ref[0, rows])

        @pl.when(do)
        def _():
            x = jnp.concatenate([r_ref[0], theirs(slice(0, W))], axis=1)
            y = mul(split(x), (ch[0], cl[0]))
            rt[0] = y[:half, :half]
            lt[0] = y[:half, half:]
            rb[0] = y[half:, :half]
            lb[0] = y[half:, half:]

        @pl.when(jnp.logical_not(do))
        def _():
            rt[0] = r_ref[0, :half]
            lt[0] = theirs(slice(0, half))

        @pl.when(jnp.logical_not(do) | (r == c))
        def _():
            rb[0] = r_ref[0, half:]
            lb[0] = theirs(slice(half, W))

        @pl.when(i < few)
        def _():
            lt_end[0] = lt[0]
            lb_end[0] = lb[0]

    whole = pl.BlockSpec((1, half, half), lambda i, s: (i, 0, 0))
    part = pl.BlockSpec((1, half, half), lambda i, s: (jnp.minimum(i, few - 1), 0, 0))
    return call(
        kernel,
        n,
        [
            pl.BlockSpec((1, W, half), lambda i, s: (i, 0, 0)),
            pl.BlockSpec((1, W, half), lambda i, s: (jnp.where(s[1] == g.C - 1, 0, i), 0, 0)),
            pl.BlockSpec(
                (1, W, half),
                lambda i, s: (jnp.where(s[1] == g.C - 1, jnp.minimum(i, few - 1), 0), 0, 0),
            ),
            pl.BlockSpec((1, W, W), lambda i, s: (lo_m + i, 0, 0)),
            pl.BlockSpec((1, W, W), lambda i, s: (lo_m + i, 0, 0)),
        ],
        [whole, whole, part, part, whole, whole],
        [shape((m, half, half)) for m in (n, n, few, few, n, n)],
        [],
        6 * n * W**3,
        12 * n * W * W,
    )(scalars, right, beyond, round_end, col_hi, col_lo)


def finish(g, k, scalars, matrix, factors, col_hi, col_lo, own, below, above, out):
    W, half, lo_m, n = g.win, g.half, g.first(k), g.count(k)

    def spec(source, wanted=None):
        size, start = g.count(source), g.first(source)

        def index(i, s):
            at = jnp.clip(lo_m + i - start, 0, size - 1)
            if wanted is not None:
                at = jnp.where(wanted(s), at, 0)
            return (at, 0, 0)

        return pl.BlockSpec((1, half, half), index)

    bottom_edge = lambda s: s[0] == g.R - 1
    top_edge = lambda s: s[0] == 0
    has_next, has_prev = below[1] is not None, above[1] is not None

    def kernel(s, h_ref, bh, bl, th, tl, qh, ql, ch, cl, lt, lb, rt, rb, *rest):
        rest = list(rest)
        take = lambda: (rest.pop(0), rest.pop(0))
        below_here, above_here = take(), take()
        below_next = take() if has_next else below_here
        above_prev = take() if has_prev else above_here
        rest.pop(0)
        o_ref, x = rest
        i = pl.program_id(0)
        r, c = k * g.R + s[0], (lo_m + i) * g.C + s[1]

        @pl.when(c < r)
        def _():
            o_ref[...] = h_ref[...]

        @pl.when(c >= r)
        def _():
            x[:half, :half] = lt[0]
            x[:half, half:] = rt[0]
            x[half:, :half] = lb[0]
            x[half:, half:] = rb[0]
            do_top = (r > 0) & flag(s, g, 1, r - 1)
            do_bottom = (r < g.N - 1) & (c > r) & flag(s, g, 1, r)

            def chosen(here, there, edge, has):
                pair = [ref[0] for ref in here]
                if has:
                    pair = [jnp.where(edge, far[0], near) for far, near in zip(there, pair)]
                return jnp.concatenate(pair, axis=1)

            @pl.when(do_top)
            def _():
                upper = chosen(above_here, above_prev, top_edge(s), has_prev)
                lower = jnp.concatenate([lt[0], rt[0]], axis=1)
                y = mul((th[0], tl[0]), split(jnp.concatenate([upper, lower], axis=0)))
                x[:half, :] = y

            @pl.when(do_bottom)
            def _():
                upper = jnp.concatenate([lb[0], rb[0]], axis=1)
                lower = chosen(below_here, below_next, bottom_edge(s), has_next)
                y = mul((bh[0], bl[0]), split(jnp.concatenate([upper, lower], axis=0)))
                x[half:, half:] = y[:, half:]

                @pl.when(c > r + 1)
                def _():
                    x[half:, :half] = y[:, :half]

            @pl.when(c == r)
            def _():
                x[:, :half] = h_ref[:, :half]

            @pl.when((c > r) & flag(s, g, 2, r))
            def _():
                x[...] = mul((qh[0], ql[0]), split(x[...]))

            do_right = (c > r) & flag(s, g, 2, c)

            @pl.when(do_right)
            def _():
                o_ref[...] = mul(split(x[...]), (ch[0], cl[0]))

            @pl.when(jnp.logical_not(do_right))
            def _():
                o_ref[...] = x[...]

    column = pl.BlockSpec((1, W, W), lambda i, s: (lo_m + i, 0, 0))
    operands = [matrix, *factors, col_hi, col_lo, *own, *below[0], *above[0]]
    in_specs = [
        pl.BlockSpec((W, W), lambda i, s: (k, lo_m + i)),
        *[pl.BlockSpec((1, half, W), lambda i, s: (k, 0, 0))] * 2,
        *[
            pl.BlockSpec(
                (1, half, W),
                lambda i, s: (jnp.maximum(k - jnp.where(s[0] == 0, 1, 0), 0), 0, 0),
            )
        ]
        * 2,
        *[pl.BlockSpec((1, W, W), lambda i, s: (k, 0, 0))] * 2,
        column,
        column,
        spec(k),
        spec(k),
        spec(k),
        spec(k),
        spec(k),
        spec(k),
        spec(k),
        spec(k),
    ]
    if has_next:
        operands += below[1]
        in_specs += [spec(k + 1, bottom_edge), spec(k + 1, bottom_edge)]
    if has_prev:
        operands += above[1]
        in_specs += [spec(k - 1, top_edge), spec(k - 1, top_edge)]
    aliases = {1 + len(operands): 0}
    operands.append(out)
    in_specs.append(pl.BlockSpec(memory_space=pl.ANY))
    return call(
        kernel,
        n,
        in_specs,
        pl.BlockSpec((W, W), lambda i, s: (k, lo_m + i)),
        shape(matrix.shape),
        [pltpu.VMEM((W, W), F32)],
        18 * n * W**3,
        24 * n * W * W,
        aliases,
    )(scalars, *operands)


def local(hessenberg, factors, active):
    rows_here, cols_here = hessenberg.shape
    phases, _, _, win = factors.shape
    R, C = lax.axis_size("row"), lax.axis_size("col")
    g = Plan(rows_here, cols_here, win, R, C)
    assert phases == 3
    p, q = lax.axis_index("row"), lax.axis_index("col")
    scalars = jnp.concatenate(
        [jnp.stack([p, q]).astype(jnp.int32), active.astype(jnp.int32).reshape(-1)]
    )

    spread = [
        [
            ((h * C + a) * C + a, (h * C + (a + d) % C) * C + a)
            for h in range(g.t)
            for a in range(C)
        ]
        for d in range(C)
    ]
    part = g.win // C

    first = lax.all_gather(factors[:1], "col", axis=2, tiled=True)
    odd_last = lax.all_gather(factors[1:], "col", axis=2, tiled=True)

    def columns(source, at, since=None):
        cut = [
            lax.dynamic_slice(
                source, (at, 0, (q + d) % C * part, 0), (1, g.kb, part, g.win)
            )[0]
            for d in range(C)
        ]
        if since is not None:
            *cut, _ = lax.optimization_barrier((*cut, since[0, :8, :128]))
        piece = jnp.where(p % C == q, cut[0], 0.0)
        for d in range(1, C):
            piece = piece + lax.ppermute(cut[d], ("row", "col"), spread[d])
        same = [piece]
        for j in range(2, R, 2):
            same.append(swap(piece, "row", j))
        same = jnp.stack(same)
        other = swap(same, "row", 1)
        return column_factors(g, scalars, same, other)

    col_factor = [columns(first, 0), columns(odd_last, 0)]
    prior = ring(odd_last[0, :, :, g.half :], "row", 1)

    finish_factors = row_factors(g, scalars, odd_last, prior)

    own, tops, bottoms = [], [], []
    for k in range(g.kb):
        left, later, right = even_first(
            g, k, scalars, hessenberg, first, *col_factor[0]
        )
        beyond = along(left, "col", -1)
        round_end = around(later, "col", -1)
        lt, lb, lt_end, lb_end, rt, rb = odd_right(
            g, k, scalars, right, beyond, round_end, *col_factor[1]
        )
        if k == 0:
            col_factor.append(columns(odd_last, 1, rb))
        lt = along(lt, "col", 1)
        lb = along(lb, "col", 1)
        lt_end = around(lt_end, "col", 1)
        lb_end = around(lb_end, "col", 1)
        lt, lb = joined(lt, lt_end), joined(lb, lb_end)
        own.append((lt, lb, rt, rb))
        rt = ring(rt, "row", -1)
        rb = ring(rb, "row", 1)
        lt = ring(lt, "row", -1)
        lb = ring(lb, "row", 1)
        tops.append((lt, rt))
        bottoms.append((lb, rb))
    out = keep_lower(g, hessenberg)
    for k in range(g.kb):
        below = (tops[k], tops[k + 1] if k + 1 < g.kb else None)
        above = (bottoms[k], bottoms[k - 1] if k > 0 else None)
        out = finish(
            g,
            k,
            scalars,
            hessenberg,
            finish_factors,
            *col_factor[2],
            own[k],
            below,
            above,
            out,
        )
    return out


def joined(straight, end):
    extra = straight.shape[0] - 1
    if not extra:
        return straight
    return straight + jnp.pad(end, ((1, 0), (0, 0), (0, 0)))


def solution(mesh):
    return jax.shard_map(
        local,
        mesh=mesh,
        in_specs=(P("row", "col"), P(None, "row", "col", None), P()),
        out_specs=P("row", "col"),
        check_vma=False,
    )
```
